1024 devices in a mesh: mat: 8 (over x), gr: 64 (over z, y), gc: 2 (over core).
Axes of the slice: x: 8, y: 8, z: 8, core: 2. Of those that a mesh axis runs over, the one named last changes fastest.
Arguments:
- iterate: bfloat16 [2, 64, 32, 7168], P(None, 'gr', ('mat', 'gc')), may hold values from -3 to 3
Outputs:
- next_iterate: bfloat16 [2, 2048, 7168], P(None, 'gr', ('mat', 'gc'))
The draws below stay inside these ranges and needn't reach their ends.
All inputs are finite; a program needn't handle non-finite values.
Results may differ from the reference program's by a relative error of at most 0.0055.
Values may be sent and summed in bfloat16 or wider, within the bound.
A program may use at most 32 MiB of HBM per device.

```python
import jax
import jax.numpy as jnp
from jax import lax

M = 2048
N = 7168
MATS = 2
RB = 32
N_GR = 64


def draw_iterate(key, part):
    base_key = jax.random.fold_in(key, 21)
    shape = (MATS, N_GR, RB, N)
    values = 0.7 * jnp.clip(jax.random.normal(base_key, shape, jnp.float32), -4.0, 4.0)
    return values.astype(jnp.bfloat16)


def setup_inputs(seed: int = 0) -> dict:
    key_of = jax.random.split(jax.random.key(seed), 2)
    iterate = draw_iterate(jax.random.fold_in(key_of[1], 71), 0)
    return {"iterate": iterate}


linear_coef = 3.4445
cubic_coef = -4.7750
quintic_coef = 2.0315


def one_matrix(blocks):
    grad = blocks.reshape(M, N)
    gram_sum = lax.dot_general(grad, grad, (((1,), (1,)), ((), ())), preferred_element_type=jnp.float32) * (1.0 / N)
    gram = gram_sum.astype(jnp.bfloat16)
    square = jnp.dot(gram, gram, preferred_element_type=jnp.float32)
    poly = (cubic_coef * gram.astype(jnp.float32) + quintic_coef * square).astype(jnp.bfloat16)
    mixed = jnp.dot(poly, grad, preferred_element_type=jnp.float32)
    result = linear_coef * grad.astype(jnp.float32) + mixed
    return result.astype(jnp.bfloat16)


def reference(iterate):
    return lax.map(one_matrix, iterate)
```

```python
import functools

import jax
import jax.numpy as jnp
from jax import lax
from jax.experimental import pallas as pl
from jax.experimental.pallas import tpu as pltpu
from jax.sharding import PartitionSpec as P

MESH = pl.DeviceIdType.MESH

linear_coef = 3.4445
cubic_coef = -4.775
quintic_coef = 2.0315


def column_cuts(width):
    cut = (width // 128 + 1) // 2 * 128
    return ((0, cut), (cut, width - cut))


class Ring:
    def __init__(self, size, me, neighbour, view, send, recv):
        self.size, self.me, self.neighbour, self.view = size, me, neighbour, view
        self.send, self.recv = send, recv

    def steps(self):
        return self.size // 2

    def has(self, step, way, q):
        return step < self.steps() or (step == self.steps() and q == way)

    def copy(self, step, way, q, index):
        turn = 1 if way == 0 else self.size - 1
        ref = self.view(lax.rem(index, self.size), q)
        return pltpu.make_async_remote_copy(
            src_ref=ref,
            dst_ref=ref,
            send_sem=self.send.at[step - 1, way, q],
            recv_sem=self.recv.at[step - 1, way, q],
            device_id={"gr": self.neighbour(lax.rem(self.me + turn, self.size))},
            device_id_type=MESH,
        )

    def sent(self, step, way, q):
        back = step - 1 if way == 1 else self.size - (step - 1)
        return self.copy(step, way, q, self.me + back)

    def arriving(self, step, way, q):
        back = step if way == 1 else self.size - step
        return self.copy(step, way, q, self.me + back)


def run_rings(rings):
    for q in range(2):
        for ring in rings:
            for way in range(2):
                if ring.has(1, way, q):
                    ring.sent(1, way, q).start()
    for step in range(1, max(r.steps() for r in rings) + 1):
        for q in range(2):
            for ring in rings:
                for way in range(2):
                    if ring.has(step, way, q):
                        ring.arriving(step, way, q).wait_recv()
                        if ring.has(step + 1, way, q):
                            ring.sent(step + 1, way, q).start()


def drain_rings(rings):
    for ring in rings:
        for step in range(1, ring.steps() + 1):
            for q in range(2):
                for way in range(2):
                    if ring.has(step, way, q):
                        ring.sent(step, way, q).wait_send()


def kernel(
    nx, nz, ny, total_cols,
    in_ref, out_ref,
    pieces, assembled, panel, partial, partial_in, gram_cols, gram_row, poly_row, swap_out, swap_in,
    a2a_send, a2a_recv, local_sem,
    pa_send, pa_recv, pb_send, pb_recv, ga_send, ga_recv, gb_send, gb_recv,
    rs_send, rs_recv, gx_send, gx_recv, px_send, px_recv, sw_send, sw_recv,
):
    x = lax.axis_index("mat")
    g = lax.axis_index("gr")
    c = lax.axis_index("gc")
    z, y = lax.div(g, ny), lax.rem(g, ny)
    rpd = in_ref.shape[1]
    block_rows, width = panel.shape[2], panel.shape[3]
    half_rows = block_rows // 2
    gram_width = gram_row.shape[2]

    def x_at(dx):
        return lax.rem(x + dx, nx)

    others = [(dx, dc) for dx in range(nx) for dc in range(2) if (dx, dc) != (0, 0)]
    barrier = pltpu.get_barrier_semaphore()
    for dx, dc in others:
        pl.semaphore_signal(
            barrier, inc=1, device_id={"mat": x_at(dx), "gc": lax.rem(c + dc, 2)}, device_id_type=MESH
        )
    for turn in (1, ny - 1):
        pl.semaphore_signal(
            barrier, inc=1, device_id={"gr": z * ny + lax.rem(y + turn, ny)}, device_id_type=MESH
        )
    for turn in (1, nz - 1):
        pl.semaphore_signal(
            barrier, inc=1, device_id={"gr": lax.rem(z + turn, nz) * ny + y}, device_id_type=MESH
        )
    pl.semaphore_wait(barrier, len(others) + 4)

    def exchange(dx, dc):
        to_x, to_c = x_at(dx), lax.rem(c + dc, 2)
        return pltpu.make_async_remote_copy(
            src_ref=in_ref.at[to_c, :, pl.ds(pl.multiple_of(to_x * width, 128), width)],
            dst_ref=pieces.at[x, c],
            send_sem=a2a_send.at[dx, dc],
            recv_sem=a2a_recv.at[dx, dc],
            device_id={"mat": to_x, "gc": to_c},
            device_id_type=MESH,
        )

    for dx, dc in others:
        exchange(dx, dc).start()
    own = pltpu.make_async_copy(
        in_ref.at[c, :, pl.ds(pl.multiple_of(x * width, 128), width)], pieces.at[x, c], local_sem
    )
    own.start()
    own.wait()
    for dx, dc in others:
        exchange(dx, dc).wait_recv()
    for k in range(nx):
        for core in range(2):
            row = (k * 2 + core) * rpd
            assembled[row : row + rpd, :] = pieces[k, core].astype(jnp.float32)
    panel[z, y] = assembled[...].astype(jnp.bfloat16)

    def gathers(buf, cuts, a_send, a_recv, b_send, b_recv):
        def rows(half):
            return pl.ds(half * half_rows, half_rows)

        def along_y(yy):
            return z * ny + yy

        def along_z(zz):
            return zz * ny + y

        first = [
            Ring(ny, y, along_y, lambda i, q: buf.at[z, i, rows(0), pl.ds(*cuts[q])], a_send.at[0], a_recv.at[0]),
            Ring(nz, z, along_z, lambda i, q: buf.at[i, y, rows(1), pl.ds(*cuts[q])], a_send.at[1], a_recv.at[1]),
        ]
        second = [
            Ring(nz, z, along_z, lambda i, q: buf.at[i, :, rows(0), pl.ds(*cuts[q])], b_send.at[0], b_recv.at[0]),
            Ring(ny, y, along_y, lambda i, q: buf.at[:, i, rows(1), pl.ds(*cuts[q])], b_send.at[1], b_recv.at[1]),
        ]
        return first, second

    panel_a, panel_b = gathers(panel, column_cuts(width), pa_send, pa_recv, pb_send, pb_recv)
    run_rings(panel_a)
    run_rings(panel_b)

    def contribute(dx):
        to_x = x_at(dx)
        return pltpu.make_async_remote_copy(
            src_ref=partial.at[to_x],
            dst_ref=partial_in.at[x],
            send_sem=rs_send.at[dx],
            recv_sem=rs_recv.at[dx],
            device_id={"mat": to_x},
            device_id_type=MESH,
        )

    far_first = sorted(range(1, nx), key=lambda dx: -min(dx, nx - dx))
    block = panel[z, y]
    for dx in far_first + [0]:
        to_x = x_at(dx)
        value = lax.dot_general(
            block,
            panel[to_x].reshape(ny * block_rows, width),
            (((1,), (1,)), ((), ())),
            preferred_element_type=jnp.float32,
        )
        if dx:
            partial[to_x] = value
            contribute(dx).start()
        else:
            gram_sum = value
    for dx in far_first:
        contribute(dx).wait_recv()
    for dx in range(1, nx):
        gram_sum = gram_sum + partial_in[x_at(dx)]
    gram = (gram_sum * (1.0 / total_cols)).astype(jnp.bfloat16)
    gram_row[x] = gram
    gram_cols[z, y] = gram

    def spread(buf, send, recv, dx, at):
        return pltpu.make_async_remote_copy(
            src_ref=buf.at[at],
            dst_ref=buf.at[at],
            send_sem=send.at[dx],
            recv_sem=recv.at[dx],
            device_id={"mat": x_at(dx)},
            device_id_type=MESH,
        )

    for dx in far_first:
        spread(gram_row, gx_send, gx_recv, dx, x).start()
    gram_a, gram_b = gathers(gram_cols, column_cuts(gram_width), ga_send, ga_recv, gb_send, gb_recv)
    run_rings(gram_a)
    run_rings(gram_b)
    for dx in far_first:
        spread(gram_row, gx_send, gx_recv, dx, x_at(nx - dx)).wait_recv()

    square = jnp.zeros((block_rows, gram_width), jnp.float32)
    for k in range(nx):
        square = square + jnp.dot(
            gram_row[k],
            gram_cols[k].reshape(ny * block_rows, gram_width),
            preferred_element_type=jnp.float32,
        )
    poly_row[x] = (cubic_coef * gram.astype(jnp.float32) + quintic_coef * square).astype(jnp.bfloat16)
    for dx in far_first:
        spread(poly_row, px_send, px_recv, dx, x).start()
    for dx in far_first:
        spread(poly_row, px_send, px_recv, dx, x_at(nx - dx)).wait_recv()

    mixed = jnp.zeros((block_rows, width), jnp.float32)
    for k in range(nx):
        mixed = mixed + jnp.dot(
            poly_row[k], panel[k].reshape(ny * block_rows, width), preferred_element_type=jnp.float32
        )
    result = linear_coef * panel[z, y].astype(jnp.float32) + mixed
    halves = [
        result[:, : width // 2].astype(jnp.bfloat16),
        result[:, width // 2 :].astype(jnp.bfloat16),
    ]
    for core in range(2):

        @pl.when(c == core)
        def _():
            out_ref[core] = halves[core]
            swap_out[...] = halves[1 - core]

    swap = pltpu.make_async_remote_copy(
        src_ref=swap_out,
        dst_ref=swap_in,
        send_sem=sw_send,
        recv_sem=sw_recv,
        device_id={"gc": 1 - c},
        device_id_type=MESH,
    )
    swap.start()
    swap.wait_recv()
    for core in range(2):

        @pl.when(c == core)
        def _():
            out_ref[1 - core] = swap_in[...]

    swap.wait_send()
    for dx, dc in others:
        exchange(dx, dc).wait_send()
    for rings in (panel_a, panel_b, gram_a, gram_b):
        drain_rings(rings)
    for dx in far_first:
        contribute(dx).wait_send()
        spread(gram_row, gx_send, gx_recv, dx, x).wait_send()
        spread(poly_row, px_send, px_recv, dx, x).wait_send()


def solution(mesh):
    nx, groups = mesh.shape["mat"], mesh.shape["gr"]
    nz = nx
    ny = groups // nz

    def body(iterate):
        mats, _, rpd, total_cols = iterate.shape
        block_rows = rpd * nx * 2
        width = total_cols // nx
        gram_width = ny * block_rows
        dma = pltpu.SemaphoreType.DMA
        y_or_z = max(ny, nz) // 2
        ring_sems = [dma((2, y_or_z, 2, 2))] * 2
        return pl.pallas_call(
            functools.partial(kernel, nx, nz, ny, total_cols),
            out_shape=jax.ShapeDtypeStruct((mats, block_rows, width // 2), jnp.bfloat16),
            in_specs=[pl.BlockSpec(memory_space=pltpu.VMEM)],
            out_specs=pl.BlockSpec(memory_space=pltpu.VMEM),
            scratch_shapes=[
                pltpu.VMEM((nx, 2, rpd, width), jnp.bfloat16),
                pltpu.VMEM((block_rows, width), jnp.float32),
                pltpu.VMEM((nz, ny, block_rows, width), jnp.bfloat16),
                pltpu.VMEM((nx, block_rows, gram_width), jnp.float32),
                pltpu.VMEM((nx, block_rows, gram_width), jnp.float32),
                pltpu.VMEM((nz, ny, block_rows, gram_width), jnp.bfloat16),
                pltpu.VMEM((nx, block_rows, gram_width), jnp.bfloat16),
                pltpu.VMEM((nx, block_rows, gram_width), jnp.bfloat16),
                pltpu.VMEM((block_rows, width // 2), jnp.bfloat16),
                pltpu.VMEM((block_rows, width // 2), jnp.bfloat16),
                dma((nx, 2)),
                dma((nx, 2)),
                dma,
            ]
            + ring_sems * 4
            + [dma((nx,))] * 6
            + [dma, dma],
            compiler_params=pltpu.CompilerParams(collective_id=0, has_side_effects=True),
        )(iterate.reshape(mats, rpd, total_cols))

    return jax.shard_map(
        body,
        mesh=mesh,
        in_specs=(P(None, "gr", ("mat", "gc"), None),),
        out_specs=P(None, "gr", ("mat", "gc")),
        check_vma=False,
    )
```

```python
import functools

import jax
import jax.numpy as jnp
from jax import lax
from jax.experimental import pallas as pl
from jax.experimental.pallas import tpu as pltpu
from jax.sharding import PartitionSpec as P

MESH = pl.DeviceIdType.MESH

linear_coef = 3.4445
cubic_coef = -4.775
quintic_coef = 2.0315


class Gather:
    def __init__(self, buf, sizes, line, line_send, line_recv, send, recv):
        self.buf, self.sizes, self.line = buf, sizes, line
        self.line_send, self.line_recv, self.send, self.recv = line_send, line_recv, send, recv
        self.half_rows = buf.shape[2] // 2

    def view(self, half, first, second):
        rows = pl.ds(half * self.half_rows, self.half_rows)
        return self.buf.at[(second, first, rows) if half == 0 else (first, second, rows)]

    def first_size(self, half):
        return self.sizes[1 - half]

    def second_size(self, half):
        return self.sizes[half]

    def first_copy(self, half, d):
        size = self.first_size(half)
        return pltpu.make_async_remote_copy(
            src_ref=self.view(half, 0, 0),
            dst_ref=self.view(half, size - d, 0),
            send_sem=self.line_send.at[half, d],
            recv_sem=self.line_recv.at[half, d],
            device_id={"gr": self.line[1 - half][d]},
            device_id_type=MESH,
        )

    def start_first(self):
        for half in range(2):
            for d in nearest_last(self.first_size(half)):
                self.first_copy(half, d).start()

    def wait_first(self, half, low, high):
        size = self.first_size(half)
        for place in range(max(low, 1), high):
            self.first_copy(half, size - place).wait_recv()

    def end_first(self):
        for half in range(2):
            for d in range(1, self.first_size(half)):
                self.first_copy(half, d).wait_send()


class RingGather(Gather):
    def chunks(self, half):
        size = self.first_size(half)
        cuts = [(0, 1), (1, size // 2), (size // 2, size)]
        return [(k, low, high) for k, (low, high) in enumerate(cuts) if low < high]

    def steps(self, half):
        return self.second_size(half) // 2

    def has(self, half, step, way, k):
        return step < self.steps(half) or (step == self.steps(half) and way == k // 2)

    def copy(self, half, step, way, chunk):
        size, (k, low, high) = self.second_size(half), chunk
        source, target = (step - 1, step) if way else ((size - step + 1) % size, size - step)
        return pltpu.make_async_remote_copy(
            src_ref=self.view(half, pl.ds(low, high - low), source),
            dst_ref=self.view(half, pl.ds(low, high - low), target),
            send_sem=self.send.at[half, step - 1, way, k],
            recv_sem=self.recv.at[half, step - 1, way, k],
            device_id={"gr": self.line[half][size - 1 if way else 1]},
            device_id_type=MESH,
        )

    def all(self):
        for half in range(2):
            for step in range(1, self.steps(half) + 1):
                for way in range(2):
                    for chunk in self.chunks(half):
                        if self.has(half, step, way, chunk[0]):
                            yield half, step, way, chunk

    def run(self):
        def start(half, step, way, chunk):
            if self.has(half, step, way, chunk[0]):
                self.copy(half, step, way, chunk).start()

        for half in range(2):
            for way in range(2):
                start(half, 1, way, self.chunks(half)[0])
        self.start_first()
        for n in range(1, 3):
            for half in range(2):
                if n < len(self.chunks(half)):
                    chunk = self.chunks(half)[n]
                    self.wait_first(half, chunk[1], chunk[2])
                    for way in range(2):
                        start(half, 1, way, chunk)
        for step in range(1, max(self.steps(0), self.steps(1)) + 1):
            for n in range(3):
                for half in range(2):
                    for way in range(2):
                        if n < len(self.chunks(half)) and self.has(half, step, way, self.chunks(half)[n][0]):
                            chunk = self.chunks(half)[n]
                            self.copy(half, step, way, chunk).wait_recv()
                            start(half, step + 1, way, chunk)

    def end(self):
        self.end_first()
        for one in self.all():
            self.copy(*one).wait_send()


class LineGather(Gather):
    def copy(self, half, d):
        size = self.second_size(half)
        return pltpu.make_async_remote_copy(
            src_ref=self.view(half, pl.ds(0, self.first_size(half)), 0),
            dst_ref=self.view(half, pl.ds(0, self.first_size(half)), size - d),
            send_sem=self.send.at[half, d],
            recv_sem=self.recv.at[half, d],
            device_id={"gr": self.line[half][d]},
            device_id_type=MESH,
        )

    def run(self):
        self.start_first()
        for half in range(2):
            self.wait_first(half, 1, self.first_size(half))
            for d in nearest_last(self.second_size(half)):
                self.copy(half, d).start()
        for half in range(2):
            for d in nearest_last(self.second_size(half)):
                self.copy(half, d).wait_recv()

    def end(self):
        self.end_first()
        for half in range(2):
            for d in range(1, self.second_size(half)):
                self.copy(half, d).wait_send()


def nearest_last(size):
    return sorted(range(1, size), key=lambda d: -min(d, size - d))


def kernel(
    nx, nz, ny, total_cols,
    in_ref, out_ref,
    pieces, assembled, panel, partial, partial_in, gram_cols, gram_row, poly_row, swap_out, swap_in,
    a2a_send, a2a_recv, local_sem,
    pa_send, pa_recv, pb_send, pb_recv, ga_send, ga_recv, gb_send, gb_recv,
    rs_send, rs_recv, gx_send, gx_recv, px_send, px_recv, sw_send, sw_recv,
):
    x = lax.axis_index("mat")
    g = lax.axis_index("gr")
    c = lax.axis_index("gc")
    z, y = lax.div(g, ny), lax.rem(g, ny)
    rpd = in_ref.shape[1]
    block_rows, width = panel.shape[2], panel.shape[3]
    gram_width = gram_row.shape[2]
    x_at = [lax.rem(x + dx, nx) for dx in range(nx)]
    c_at = [c, 1 - c]
    line = (
        [lax.rem(z + dz, nz) * ny + y for dz in range(nz)],
        [z * ny + lax.rem(y + dy, ny) for dy in range(ny)],
    )
    place_z = [lax.rem(x_at[dx] + nz - z, nz) for dx in range(nx)]
    place_y = [lax.rem(k + ny - y, ny) for k in range(ny)]

    def row_block(buf, dx):
        return jnp.concatenate([buf[place_z[dx], place_y[k]] for k in range(ny)], axis=0)

    others = [(dx, dc) for dx in nearest_last(nx) + [0] for dc in range(2) if (dx, dc) != (0, 0)]
    barrier = pltpu.get_barrier_semaphore()
    for dx, dc in others:
        pl.semaphore_signal(
            barrier, inc=1, device_id={"mat": x_at[dx], "gc": c_at[dc]}, device_id_type=MESH
        )
    for axis in range(2):
        for to in line[axis][1:]:
            pl.semaphore_signal(barrier, inc=1, device_id={"gr": to}, device_id_type=MESH)
    pl.semaphore_wait(barrier, len(others) + nz - 1 + ny - 1)

    def exchange(dx, dc):
        to_x, to_c = x_at[dx], c_at[dc]
        return pltpu.make_async_remote_copy(
            src_ref=in_ref.at[to_c, :, pl.ds(pl.multiple_of(to_x * width, 128), width)],
            dst_ref=pieces.at[x, c],
            send_sem=a2a_send.at[dx, dc],
            recv_sem=a2a_recv.at[dx, dc],
            device_id={"mat": to_x, "gc": to_c},
            device_id_type=MESH,
        )

    for dx, dc in others:
        exchange(dx, dc).start()
    own = pltpu.make_async_copy(
        in_ref.at[c, :, pl.ds(pl.multiple_of(x * width, 128), width)], pieces.at[x, c], local_sem
    )
    own.start()
    own.wait()
    for dx, dc in others:
        exchange(dx, dc).wait_recv()
    for k in range(nx):
        for core in range(2):
            row = (k * 2 + core) * rpd
            assembled[row : row + rpd, :] = pieces[k, core].astype(jnp.float32)
    block = assembled[...].astype(jnp.bfloat16)
    panel[0, 0] = block

    panel_gather = RingGather(panel, (nz, ny), line, pa_send, pa_recv, pb_send, pb_recv)
    panel_gather.run()

    def contribute(dx):
        return pltpu.make_async_remote_copy(
            src_ref=partial.at[dx],
            dst_ref=partial_in.at[nx - dx],
            send_sem=rs_send.at[dx],
            recv_sem=rs_recv.at[dx],
            device_id={"mat": x_at[dx]},
            device_id_type=MESH,
        )

    far_first = nearest_last(nx)
    for dx in far_first + [0]:
        value = lax.dot_general(
            block, row_block(panel, dx), (((1,), (1,)), ((), ())), preferred_element_type=jnp.float32
        )
        if dx:
            partial[dx] = value
            contribute(dx).start()
        else:
            gram_sum = value
    for dx in far_first:
        contribute(dx).wait_recv()
        gram_sum = gram_sum + partial_in[nx - dx]
    gram = (gram_sum * (1.0 / total_cols)).astype(jnp.bfloat16)
    gram_row[0] = gram
    gram_cols[0, 0] = gram

    def spread(buf, send, recv, dx):
        return pltpu.make_async_remote_copy(
            src_ref=buf.at[0],
            dst_ref=buf.at[nx - dx],
            send_sem=send.at[dx],
            recv_sem=recv.at[dx],
            device_id={"mat": x_at[dx]},
            device_id_type=MESH,
        )

    for dx in far_first:
        spread(gram_row, gx_send, gx_recv, dx).start()
    gram_gather = LineGather(gram_cols, (nz, ny), line, ga_send, ga_recv, gb_send, gb_recv)
    gram_gather.run()
    for dx in far_first:
        spread(gram_row, gx_send, gx_recv, dx).wait_recv()

    square = jnp.zeros((block_rows, gram_width), jnp.float32)
    for dx in range(nx):
        square = square + jnp.dot(gram_row[dx], row_block(gram_cols, dx), preferred_element_type=jnp.float32)
    poly_row[0] = (cubic_coef * gram.astype(jnp.float32) + quintic_coef * square).astype(jnp.bfloat16)
    for dx in far_first:
        spread(poly_row, px_send, px_recv, dx).start()

    mixed = jnp.zeros((block_rows, width), jnp.float32)
    for dx in [0] + far_first[::-1]:
        if dx:
            spread(poly_row, px_send, px_recv, nx - dx).wait_recv()
        mixed = mixed + jnp.dot(poly_row[dx], row_block(panel, dx), preferred_element_type=jnp.float32)
    result = linear_coef * block.astype(jnp.float32) + mixed
    halves = [
        result[:, : width // 2].astype(jnp.bfloat16),
        result[:, width // 2 :].astype(jnp.bfloat16),
    ]
    for core in range(2):

        @pl.when(c == core)
        def _():
            out_ref[core] = halves[core]
            swap_out[...] = halves[1 - core]

    swap = pltpu.make_async_remote_copy(
        src_ref=swap_out,
        dst_ref=swap_in,
        send_sem=sw_send,
        recv_sem=sw_recv,
        device_id={"gc": 1 - c},
        device_id_type=MESH,
    )
    swap.start()
    for dx, dc in others:
        exchange(dx, dc).wait_send()
    panel_gather.end()
    gram_gather.end()
    for dx in far_first:
        contribute(dx).wait_send()
        spread(gram_row, gx_send, gx_recv, dx).wait_send()
        spread(poly_row, px_send, px_recv, dx).wait_send()
    swap.wait_recv()
    for core in range(2):

        @pl.when(c == core)
        def _():
            out_ref[1 - core] = swap_in[...]

    swap.wait_send()


def solution(mesh):
    nx, groups = mesh.shape["mat"], mesh.shape["gr"]
    nz = nx
    ny = groups // nz

    def body(iterate):
        mats, _, rpd, total_cols = iterate.shape
        block_rows = rpd * nx * 2
        width = total_cols // nx
        gram_width = ny * block_rows
        dma = pltpu.SemaphoreType.DMA
        long = max(ny, nz)
        return pl.pallas_call(
            functools.partial(kernel, nx, nz, ny, total_cols),
            out_shape=jax.ShapeDtypeStruct((mats, block_rows, width // 2), jnp.bfloat16),
            in_specs=[pl.BlockSpec(memory_space=pl.ANY)],
            out_specs=pl.BlockSpec(memory_space=pltpu.VMEM),
            scratch_shapes=[
                pltpu.VMEM((nx, 2, rpd, width), jnp.bfloat16),
                pltpu.VMEM((block_rows, width), jnp.float32),
                pltpu.VMEM((nz, ny, block_rows, width), jnp.bfloat16),
                pltpu.VMEM((nx, block_rows, gram_width), jnp.float32),
                pltpu.VMEM((nx, block_rows, gram_width), jnp.float32),
                pltpu.VMEM((nz, ny, block_rows, gram_width), jnp.bfloat16),
                pltpu.VMEM((nx, block_rows, gram_width), jnp.bfloat16),
                pltpu.VMEM((nx, block_rows, gram_width), jnp.bfloat16),
                pltpu.VMEM((block_rows, width // 2), jnp.bfloat16),
                pltpu.VMEM((block_rows, width // 2), jnp.bfloat16),
                dma((nx, 2)),
                dma((nx, 2)),
                dma,
            ]
            + [dma((2, long))] * 2
            + [dma((2, long // 2, 2, 3))] * 2
            + [dma((2, long))] * 4
            + [dma((nx,))] * 6
            + [dma, dma],
            compiler_params=pltpu.CompilerParams(collective_id=0, has_side_effects=True),
        )(iterate.reshape(mats, rpd, total_cols))

    return jax.shard_map(
        body,
        mesh=mesh,
        in_specs=(P(None, "gr", ("mat", "gc"), None),),
        out_specs=P(None, "gr", ("mat", "gc")),
        check_vma=False,
    )
```

```python
import functools

import jax
import jax.numpy as jnp
from jax import lax
from jax.experimental import pallas as pl
from jax.experimental.pallas import tpu as pltpu
from jax.sharding import PartitionSpec as P

MESH = pl.DeviceIdType.MESH

linear_coef = 3.4445
cubic_coef = -4.775
quintic_coef = 2.0315


def nearest_first(size):
    return sorted(range(size), key=lambda d: 2 * d - 1 if d <= size // 2 else 2 * (size - d))


def slot_of(d, size):
    return nearest_first(size).index(d % size)


def traced_slot(d, size):
    return jnp.maximum(jnp.minimum(2 * d - 1, 2 * (size - d)), 0)


def hop(size, d):
    if size == 8 and d in (0, 3, 4, 5):
        return {3: (-2, 1, None), 5: (2, -1, None), 4: (-2, 2, 0), 0: (2, -2, 1)}[d]
    return 0, d, None


def at_once(size):
    return (2, 6, 1, 7) if size == 8 else tuple(range(1, size))


def passed_on(size):
    return (3, 5, 4, 0) if size == 8 else ()


def line_copies(size):
    return at_once(size) + passed_on(size)


def arriving(size, place):
    return [d for d in line_copies(size) if (hop(size, d)[0] - hop(size, d)[1] - place) % size == 0]


class Gather:
    def __init__(self, buf, sizes, line, line_send, line_recv, send, recv):
        self.buf, self.sizes, self.line = buf, sizes, line
        self.line_send, self.line_recv, self.send, self.recv = line_send, line_recv, send, recv
        self.half_rows = buf.shape[2] // 2

    def view(self, half, first, second, part=None):
        rows = pl.ds(half * self.half_rows, self.half_rows)
        width = self.buf.shape[3]
        cut = (width // 128 + 1) // 2 * 128
        columns = pl.ds(0, width) if part is None else pl.ds(cut, width - cut) if part else pl.ds(0, cut)
        return self.buf.at[(second, first, rows, columns) if half == 0 else (first, second, rows, columns)]

    def first_size(self, half):
        return self.sizes[1 - half]

    def second_size(self, half):
        return self.sizes[half]

    def first_copy(self, half, d):
        size = self.first_size(half)
        source, to, part = hop(size, d)
        return pltpu.make_async_remote_copy(
            src_ref=self.view(half, slot_of(source, size), 0, part),
            dst_ref=self.view(half, slot_of(source - to, size), 0, part),
            send_sem=self.line_send.at[half, d],
            recv_sem=self.line_recv.at[half, d],
            device_id={"gr": self.line[1 - half][to % size]},
            device_id_type=MESH,
        )

    def start_first(self):
        for n in range(max(self.sizes)):
            for half in range(2):
                now = at_once(self.first_size(half))
                if n < len(now):
                    self.first_copy(half, now[n]).start()

    def wait_first(self, low, high):
        for half in range(2):
            size = self.first_size(half)
            for place in nearest_first(size)[low:high]:
                for d in arriving(size, place):
                    self.first_copy(half, d).wait_recv()

    def pass_on_first(self):
        for half in range(2):
            for d in passed_on(self.first_size(half)):
                self.first_copy(half, d).start()

    def end_first(self):
        for half in range(2):
            for d in line_copies(self.first_size(half)):
                self.first_copy(half, d).wait_send()


class RingGather(Gather):
    def chunks(self, half):
        size = self.first_size(half)
        cuts = [(0, 1), (1, min(3, size)), (3, min(5, size)), (5, min(7, size)), (7, size)]
        return [(k, low, high) for k, (low, high) in enumerate(cuts) if low < high]

    def steps(self, half):
        return self.second_size(half) // 2

    def has(self, half, step, way, k):
        return step < self.steps(half) or (step == self.steps(half) and way == (k in (2, 3)))

    def copy(self, half, step, way, chunk):
        size, (k, low, high) = self.second_size(half), chunk
        source, target = (step - 1, step) if way else (1 - step, -step)
        source, target = slot_of(source, size), slot_of(target, size)
        return pltpu.make_async_remote_copy(
            src_ref=self.view(half, pl.ds(low, high - low), source),
            dst_ref=self.view(half, pl.ds(low, high - low), target),
            send_sem=self.send.at[half, step - 1, way, k],
            recv_sem=self.recv.at[half, step - 1, way, k],
            device_id={"gr": self.line[half][size - 1 if way else 1]},
            device_id_type=MESH,
        )

    def all(self):
        for half in range(2):
            for step in range(1, self.steps(half) + 1):
                for way in range(2):
                    for chunk in self.chunks(half):
                        if self.has(half, step, way, chunk[0]):
                            yield half, step, way, chunk

    def begin(self, n):
        for half in range(2):
            for way in range(2):
                if n < len(self.chunks(half)) and self.has(half, 1, way, n):
                    self.copy(half, 1, way, self.chunks(half)[n]).start()

    def forward(self, step, n):
        for half in range(2):
            for way in range(2):
                if n < len(self.chunks(half)) and self.has(half, step, way, n):
                    chunk = self.chunks(half)[n]
                    self.copy(half, step, way, chunk).wait_recv()
                    if self.has(half, step + 1, way, n):
                        self.copy(half, step + 1, way, chunk).start()

    def run(self, ready):
        self.start_first()
        self.begin(0)
        self.wait_first(3, 5)
        self.pass_on_first()
        self.wait_first(1, 3)
        self.begin(1)
        self.begin(2)
        self.forward(1, 0)
        self.wait_first(5, 7)
        self.begin(3)
        self.wait_first(7, 8)
        self.begin(4)
        for step in range(1, max(self.steps(0), self.steps(1)) + 1):
            for n in range(step == 1, 5):
                self.forward(step, n)
            for half in range(2):
                if step <= self.steps(half):
                    for d in sorted({0, step, self.second_size(half) - step} if step == 1 else {step, self.second_size(half) - step}):
                        ready(half, d)

    def end(self):
        self.end_first()
        for one in self.all():
            self.copy(*one).wait_send()


class HopGather(Gather):
    def chunks(self, half):
        size = self.first_size(half)
        return [(0, min(5, size)), (5, size)][: 1 + (size > 5)]

    def copy(self, half, d, k):
        size = self.second_size(half)
        source, to, part = hop(size, d)
        low, high = self.chunks(half)[k]
        return pltpu.make_async_remote_copy(
            src_ref=self.view(half, pl.ds(low, high - low), slot_of(source, size), part),
            dst_ref=self.view(half, pl.ds(low, high - low), slot_of(source - to, size), part),
            send_sem=self.send.at[half, d, k],
            recv_sem=self.recv.at[half, d, k],
            device_id={"gr": self.line[half][to % size]},
            device_id_type=MESH,
        )

    def run(self):
        waited = set()

        def wait(half, d, k):
            if (half, d, k) not in waited:
                waited.add((half, d, k))
                self.copy(half, d, k).wait_recv()

        self.start_first()
        self.wait_first(3, 5)
        self.pass_on_first()
        self.wait_first(1, 3)
        for k in range(2):
            if k:
                self.wait_first(5, 8)
            for half in range(2):
                if k < len(self.chunks(half)):
                    for d in at_once(self.second_size(half)):
                        self.copy(half, d, k).start()
        for k in range(2):
            for half in range(2):
                size = self.second_size(half)
                for d in passed_on(size):
                    for before in arriving(size, hop(size, d)[0]):
                        wait(half, before, k)
                    self.copy(half, d, k).start()
        for half in range(2):
            for k in range(len(self.chunks(half))):
                for d in line_copies(self.second_size(half)):
                    wait(half, d, k)

    def end(self):
        self.end_first()
        for half in range(2):
            for k in range(len(self.chunks(half))):
                for d in line_copies(self.second_size(half)):
                    self.copy(half, d, k).wait_send()


def nearest_last(size):
    return sorted(range(1, size), key=lambda d: -min(d, size - d))


def kernel(
    nx, nz, ny, total_cols,
    in_ref, out_ref,
    pieces, assembled, panel, partial, partial_in, gram_cols, gram_row, poly_row, swap_out, swap_in,
    a2a_send, a2a_recv, local_sem,
    pa_send, pa_recv, pb_send, pb_recv, ga_send, ga_recv, gb_send, gb_recv,
    rs_send, rs_recv, gx_send, gx_recv, px_send, px_recv, sw_send, sw_recv,
):
    x = lax.axis_index("mat")
    g = lax.axis_index("gr")
    c = lax.axis_index("gc")
    z, y = lax.div(g, ny), lax.rem(g, ny)
    rpd = in_ref.shape[1]
    block_rows, width = panel.shape[2], panel.shape[3]
    gram_width = gram_row.shape[2]
    x_at = [lax.rem(x + dx, nx) for dx in range(nx)]
    c_at = [c, 1 - c]
    line = (
        [lax.rem(z + dz, nz) * ny + y for dz in range(nz)],
        [z * ny + lax.rem(y + dy, ny) for dy in range(ny)],
    )
    half_rows = block_rows // 2
    slot_z = [traced_slot(lax.rem(k + nz - z, nz), nz) for k in range(nz)]
    slot_y = [traced_slot(lax.rem(k + ny - y, ny), ny) for k in range(ny)]
    block_z = [traced_slot(lax.rem(x_at[dx] + nz - z, nz), nz) for dx in range(nx)]
    block_y = [traced_slot(lax.rem(x_at[dx] + ny - y, ny), ny) for dx in range(nx)]

    def half_block(buf, half, slot):
        if half == 0:
            return jnp.concatenate([buf[slot, k, :half_rows] for k in slot_y], axis=0)
        return jnp.concatenate([buf[k, slot, half_rows:] for k in slot_z], axis=0)

    def row_block(buf, dx):
        return jnp.concatenate([half_block(buf, 0, block_z[dx]), half_block(buf, 1, block_y[dx])], axis=0)

    others = [(dx, dc) for dx in nearest_last(nx) + [0] for dc in range(2) if (dx, dc) != (0, 0)]
    barrier = pltpu.get_barrier_semaphore()
    for dx, dc in others:
        pl.semaphore_signal(
            barrier, inc=1, device_id={"mat": x_at[dx], "gc": c_at[dc]}, device_id_type=MESH
        )
    for axis in range(2):
        for to in line[axis][1:]:
            pl.semaphore_signal(barrier, inc=1, device_id={"gr": to}, device_id_type=MESH)
    pl.semaphore_wait(barrier, len(others) + nz - 1 + ny - 1)

    def exchange(dx, dc):
        to_x, to_c = x_at[dx], c_at[dc]
        return pltpu.make_async_remote_copy(
            src_ref=in_ref.at[to_c, :, pl.ds(pl.multiple_of(to_x * width, 128), width)],
            dst_ref=pieces.at[x, c],
            send_sem=a2a_send.at[dx, dc],
            recv_sem=a2a_recv.at[dx, dc],
            device_id={"mat": to_x, "gc": to_c},
            device_id_type=MESH,
        )

    for dx, dc in others:
        exchange(dx, dc).start()
    own = pltpu.make_async_copy(
        in_ref.at[c, :, pl.ds(pl.multiple_of(x * width, 128), width)], pieces.at[x, c], local_sem
    )
    own.start()
    own.wait()
    for dx, dc in others:
        exchange(dx, dc).wait_recv()
    for k in range(nx):
        for core in range(2):
            row = (k * 2 + core) * rpd
            assembled[row : row + rpd, :] = pieces[k, core].astype(jnp.float32)
    block = assembled[...].astype(jnp.bfloat16)
    panel[0, 0] = block

    def owner(half, d):
        return lax.rem(z + d, nz) if half == 0 else lax.rem(y + d, ny)

    def contribute(half, d):
        return pltpu.make_async_remote_copy(
            src_ref=partial.at[half, d],
            dst_ref=partial_in.at[half, x],
            send_sem=rs_send.at[half, d],
            recv_sem=rs_recv.at[half, x],
            device_id={"mat": owner(half, d)},
            device_id_type=MESH,
        )

    def ready(half, d):
        partial[half, d] = lax.dot_general(
            block,
            half_block(panel, half, slot_of(d, nx)),
            (((1,), (1,)), ((), ())),
            preferred_element_type=jnp.float32,
        )

        @pl.when(owner(half, d) != x)
        def _():
            contribute(half, d).start()

        @pl.when(owner(half, d) == x)
        def _():
            partial_in[half, x] = partial[half, d]

    panel_gather = RingGather(panel, (nz, ny), line, pa_send, pa_recv, pb_send, pb_recv)
    panel_gather.run(ready)

    far_first = nearest_last(nx)
    sums = []
    for half in range(2):
        for dx in far_first:
            pltpu.make_async_remote_copy(
                src_ref=partial_in.at[half, x_at[dx]],
                dst_ref=partial_in.at[half, x_at[dx]],
                send_sem=rs_send.at[half, dx],
                recv_sem=rs_recv.at[half, x_at[dx]],
                device_id={"mat": x_at[dx]},
                device_id_type=MESH,
            ).wait_recv()
        total = partial_in[half, 0]
        for k in range(1, nx):
            total = total + partial_in[half, k]
        sums.append(total)
    gram_sum = jnp.concatenate(sums, axis=1)
    gram = (gram_sum * (1.0 / total_cols)).astype(jnp.bfloat16)
    gram_row[0] = gram
    gram_cols[0, 0] = gram

    def spread(buf, send, recv, dx):
        return pltpu.make_async_remote_copy(
            src_ref=buf.at[0],
            dst_ref=buf.at[nx - dx],
            send_sem=send.at[dx],
            recv_sem=recv.at[dx],
            device_id={"mat": x_at[dx]},
            device_id_type=MESH,
        )

    for dx in far_first:
        spread(gram_row, gx_send, gx_recv, dx).start()
    gram_gather = HopGather(gram_cols, (nz, ny), line, ga_send, ga_recv, gb_send, gb_recv)
    gram_gather.run()
    for dx in far_first:
        spread(gram_row, gx_send, gx_recv, dx).wait_recv()

    square = jnp.zeros((block_rows, gram_width), jnp.float32)
    for dx in range(nx):
        square = square + jnp.dot(gram_row[dx], row_block(gram_cols, dx), preferred_element_type=jnp.float32)
    poly_row[0] = (cubic_coef * gram.astype(jnp.float32) + quintic_coef * square).astype(jnp.bfloat16)
    for dx in far_first:
        spread(poly_row, px_send, px_recv, dx).start()

    mixed = jnp.zeros((block_rows, width), jnp.float32)
    for dx in [0] + far_first[::-1]:
        if dx:
            spread(poly_row, px_send, px_recv, nx - dx).wait_recv()
        mixed = mixed + jnp.dot(poly_row[dx], row_block(panel, dx), preferred_element_type=jnp.float32)
    result = linear_coef * block.astype(jnp.float32) + mixed
    halves = [
        result[:, : width // 2].astype(jnp.bfloat16),
        result[:, width // 2 :].astype(jnp.bfloat16),
    ]
    for core in range(2):

        @pl.when(c == core)
        def _():
            out_ref[core] = halves[core]
            swap_out[...] = halves[1 - core]

    swap = pltpu.make_async_remote_copy(
        src_ref=swap_out,
        dst_ref=swap_in,
        send_sem=sw_send,
        recv_sem=sw_recv,
        device_id={"gc": 1 - c},
        device_id_type=MESH,
    )
    swap.start()
    for dx, dc in others:
        exchange(dx, dc).wait_send()
    panel_gather.end()
    gram_gather.end()
    for half in range(2):
        for d in range(nx):

            @pl.when(owner(half, d) != x)
            def _():
                contribute(half, d).wait_send()

    for dx in far_first:
        spread(gram_row, gx_send, gx_recv, dx).wait_send()
        spread(poly_row, px_send, px_recv, dx).wait_send()
    swap.wait_recv()
    for core in range(2):

        @pl.when(c == core)
        def _():
            out_ref[1 - core] = swap_in[...]

    swap.wait_send()


def solution(mesh):
    nx, groups = mesh.shape["mat"], mesh.shape["gr"]
    nz = nx
    ny = groups // nz

    def body(iterate):
        mats, _, rpd, total_cols = iterate.shape
        block_rows = rpd * nx * 2
        width = total_cols // nx
        gram_width = ny * block_rows
        dma = pltpu.SemaphoreType.DMA
        long = max(ny, nz)
        return pl.pallas_call(
            functools.partial(kernel, nx, nz, ny, total_cols),
            out_shape=jax.ShapeDtypeStruct((mats, block_rows, width // 2), jnp.bfloat16),
            in_specs=[pl.BlockSpec(memory_space=pl.ANY)],
            out_specs=pl.BlockSpec(memory_space=pltpu.VMEM),
            scratch_shapes=[
                pltpu.VMEM((nx, 2, rpd, width), jnp.bfloat16),
                pltpu.VMEM((block_rows, width), jnp.float32),
                pltpu.VMEM((nz, ny, block_rows, width), jnp.bfloat16),
                pltpu.VMEM((2, nx, block_rows, gram_width // 2), jnp.float32),
                pltpu.VMEM((2, nx, block_rows, gram_width // 2), jnp.float32),
                pltpu.VMEM((nz, ny, block_rows, gram_width), jnp.bfloat16),
                pltpu.VMEM((nx, block_rows, gram_width), jnp.bfloat16),
                pltpu.VMEM((nx, block_rows, gram_width), jnp.bfloat16),
                pltpu.VMEM((block_rows, width // 2), jnp.bfloat16),
                pltpu.VMEM((block_rows, width // 2), jnp.bfloat16),
                dma((nx, 2)),
                dma((nx, 2)),
                dma,
            ]
            + [dma((2, long))] * 2
            + [dma((2, long // 2, 2, 5))] * 2
            + [dma((2, long))] * 2
            + [dma((2, long, 2))] * 2
            + [dma((2, nx))] * 2
            + [dma((nx,))] * 4
            + [dma, dma],
            compiler_params=pltpu.CompilerParams(collective_id=0, has_side_effects=True),
        )(iterate.reshape(mats, rpd, total_cols))

    return jax.shard_map(
        body,
        mesh=mesh,
        in_specs=(P(None, "gr", ("mat", "gc"), None),),
        out_specs=P(None, "gr", ("mat", "gc")),
        check_vma=False,
    )
```

```python
import functools

import jax
import jax.numpy as jnp
from jax import lax
from jax.experimental import pallas as pl
from jax.experimental.pallas import tpu as pltpu
from jax.sharding import PartitionSpec as P

MESH = pl.DeviceIdType.MESH

linear_coef = 3.4445
cubic_coef = -4.775
quintic_coef = 2.0315


def nearest_first(size):
    return sorted(range(size), key=lambda d: 2 * d - 1 if d <= size // 2 else 2 * (size - d))


def slot_of(d, size):
    return nearest_first(size).index(d % size)


def traced_slot(d, size):
    return jnp.maximum(jnp.minimum(2 * d - 1, 2 * (size - d)), 0)


def hop(size, d):
    if size == 8 and d in (0, 3, 4, 5):
        return {3: (-2, 1, None), 5: (2, -1, None), 4: (-2, 2, 0), 0: (2, -2, 1)}[d]
    return 0, d, None


def at_once(size):
    return (2, 6, 1, 7) if size == 8 else tuple(range(1, size))


def passed_on(size):
    return (3, 5, 4, 0) if size == 8 else ()


def line_copies(size):
    return at_once(size) + passed_on(size)


def arriving(size, place):
    return [d for d in line_copies(size) if (hop(size, d)[0] - hop(size, d)[1] - place) % size == 0]


class Gather:
    def __init__(self, buf, sizes, line, line_send, line_recv, send, recv):
        self.buf, self.sizes, self.line = buf, sizes, line
        self.line_send, self.line_recv, self.send, self.recv = line_send, line_recv, send, recv
        self.half_rows = buf.shape[2] // 2

    def view(self, half, first, second, part=None):
        rows = pl.ds(half * self.half_rows, self.half_rows)
        width = self.buf.shape[3]
        cut = (width // 128 + 1) // 2 * 128
        columns = pl.ds(0, width) if part is None else pl.ds(cut, width - cut) if part else pl.ds(0, cut)
        return self.buf.at[(second, first, rows, columns) if half == 0 else (first, second, rows, columns)]

    def first_size(self, half):
        return self.sizes[1 - half]

    def second_size(self, half):
        return self.sizes[half]

    def first_copy(self, half, d):
        size = self.first_size(half)
        source, to, part = hop(size, d)
        return pltpu.make_async_remote_copy(
            src_ref=self.view(half, slot_of(source, size), 0, part),
            dst_ref=self.view(half, slot_of(source - to, size), 0, part),
            send_sem=self.line_send.at[half, d],
            recv_sem=self.line_recv.at[half, d],
            device_id={"gr": self.line[1 - half][to % size]},
            device_id_type=MESH,
        )

    def start_first(self):
        for n in range(max(self.sizes)):
            for half in range(2):
                now = at_once(self.first_size(half))
                if n < len(now):
                    self.first_copy(half, now[n]).start()

    def wait_first(self, low, high):
        for half in range(2):
            size = self.first_size(half)
            for place in nearest_first(size)[low:high]:
                for d in arriving(size, place):
                    self.first_copy(half, d).wait_recv()

    def pass_on_first(self):
        for half in range(2):
            for d in passed_on(self.first_size(half)):
                self.first_copy(half, d).start()

    def end_first(self):
        for half in range(2):
            for d in line_copies(self.first_size(half)):
                self.first_copy(half, d).wait_send()


class RingGather(Gather):
    def chunks(self, half):
        size = self.first_size(half)
        cuts = [(0, 1), (1, min(3, size)), (3, min(5, size)), (5, min(7, size)), (7, size)]
        return [(k, low, high) for k, (low, high) in enumerate(cuts) if low < high]

    def steps(self, half):
        return self.second_size(half) // 2

    def has(self, half, step, way, k):
        return step < self.steps(half) or (step == self.steps(half) and way == (k in (2, 3)))

    def copy(self, half, step, way, chunk):
        size, (k, low, high) = self.second_size(half), chunk
        source, target = (step - 1, step) if way else (1 - step, -step)
        source, target = slot_of(source, size), slot_of(target, size)
        return pltpu.make_async_remote_copy(
            src_ref=self.view(half, pl.ds(low, high - low), source),
            dst_ref=self.view(half, pl.ds(low, high - low), target),
            send_sem=self.send.at[half, step - 1, way, k],
            recv_sem=self.recv.at[half, step - 1, way, k],
            device_id={"gr": self.line[half][size - 1 if way else 1]},
            device_id_type=MESH,
        )

    def all(self):
        for half in range(2):
            for step in range(1, self.steps(half) + 1):
                for way in range(2):
                    for chunk in self.chunks(half):
                        if self.has(half, step, way, chunk[0]):
                            yield half, step, way, chunk

    def begin(self, n):
        for half in range(2):
            for way in range(2):
                if n < len(self.chunks(half)) and self.has(half, 1, way, n):
                    self.copy(half, 1, way, self.chunks(half)[n]).start()

    def forward(self, step, n):
        for half in range(2):
            for way in range(2):
                if n < len(self.chunks(half)) and self.has(half, step, way, n):
                    chunk = self.chunks(half)[n]
                    self.copy(half, step, way, chunk).wait_recv()
                    if self.has(half, step + 1, way, n):
                        self.copy(half, step + 1, way, chunk).start()

    def run(self, ready):
        self.start_first()
        self.begin(0)
        self.wait_first(3, 5)
        self.pass_on_first()
        self.wait_first(1, 3)
        self.begin(1)
        self.begin(2)
        self.forward(1, 0)
        self.wait_first(5, 7)
        self.begin(3)
        self.wait_first(7, 8)
        self.begin(4)
        for step in range(1, max(self.steps(0), self.steps(1)) + 1):
            for n in range(step == 1, 5):
                self.forward(step, n)
            for half in range(2):
                if step <= self.steps(half):
                    for d in sorted({0, step, self.second_size(half) - step} if step == 1 else {step, self.second_size(half) - step}):
                        ready(half, d)

    def end(self):
        self.end_first()
        for one in self.all():
            self.copy(*one).wait_send()


class LineGather(Gather):
    relay = False

    def first_copy(self, half, d):
        size = self.first_size(half)
        return pltpu.make_async_remote_copy(
            src_ref=self.view(half, 0, 0),
            dst_ref=self.view(half, slot_of(-d, size), 0),
            send_sem=self.line_send.at[half, d],
            recv_sem=self.line_recv.at[half, d],
            device_id={"gr": self.line[1 - half][d]},
            device_id_type=MESH,
        )

    def plan(self, half):
        size = self.second_size(half)
        if self.relay and size == 8:
            return (2, 6, 3, 5, 1, 7), ((4, 2), (0, 6))
        return tuple(nearest_last(size)), ()

    def copy(self, half, d):
        size = self.second_size(half)
        relayed = [one for one, _ in self.plan(half)[1]]
        source, to, part = hop(size, d) if d in relayed else (0, d, None)
        return pltpu.make_async_remote_copy(
            src_ref=self.view(half, pl.ds(0, self.first_size(half)), slot_of(source, size), part),
            dst_ref=self.view(half, pl.ds(0, self.first_size(half)), slot_of(source - to, size), part),
            send_sem=self.send.at[half, d],
            recv_sem=self.recv.at[half, d],
            device_id={"gr": self.line[half][to % size]},
            device_id_type=MESH,
        )

    def run(self):
        for half in range(2):
            for d in nearest_last(self.first_size(half)):
                self.first_copy(half, d).start()
        for half in range(2):
            for d in range(1, self.first_size(half)):
                self.first_copy(half, d).wait_recv()
            for d in self.plan(half)[0]:
                self.copy(half, d).start()
        for half in range(2):
            for d, before in self.plan(half)[1]:
                self.copy(half, before).wait_recv()
                self.copy(half, d).start()
        for half in range(2):
            now, later = self.plan(half)
            relays = [before for _, before in later]
            for d in now + tuple(d for d, _ in later):
                if d not in relays:
                    self.copy(half, d).wait_recv()

    def end(self):
        for half in range(2):
            for d in range(1, self.first_size(half)):
                self.first_copy(half, d).wait_send()
            now, later = self.plan(half)
            for d in now + tuple(d for d, _ in later):
                self.copy(half, d).wait_send()


def nearest_last(size):
    return sorted(range(1, size), key=lambda d: -min(d, size - d))


def kernel(
    nx, nz, ny, total_cols,
    in_ref, out_ref,
    pieces, assembled, panel, partial, partial_in, gram_cols, gram_row, poly_row, swap_out, swap_in,
    a2a_send, a2a_recv, local_sem,
    pa_send, pa_recv, pb_send, pb_recv, ga_send, ga_recv, gb_send, gb_recv,
    rs_send, rs_recv, gx_send, gx_recv, px_send, px_recv, sw_send, sw_recv,
):
    x = lax.axis_index("mat")
    g = lax.axis_index("gr")
    c = lax.axis_index("gc")
    z, y = lax.div(g, ny), lax.rem(g, ny)
    rpd = in_ref.shape[1]
    block_rows, width = panel.shape[2], panel.shape[3]
    gram_width = gram_row.shape[2]
    x_at = [lax.rem(x + dx, nx) for dx in range(nx)]
    c_at = [c, 1 - c]
    line = (
        [lax.rem(z + dz, nz) * ny + y for dz in range(nz)],
        [z * ny + lax.rem(y + dy, ny) for dy in range(ny)],
    )
    half_rows = block_rows // 2
    slot_z = [traced_slot(lax.rem(k + nz - z, nz), nz) for k in range(nz)]
    slot_y = [traced_slot(lax.rem(k + ny - y, ny), ny) for k in range(ny)]
    block_z = [traced_slot(lax.rem(x_at[dx] + nz - z, nz), nz) for dx in range(nx)]
    block_y = [traced_slot(lax.rem(x_at[dx] + ny - y, ny), ny) for dx in range(nx)]

    def half_block(buf, half, slot, columns=slice(None)):
        if half == 0:
            return jnp.concatenate([buf[slot, k, :half_rows, columns] for k in slot_y], axis=0)
        return jnp.concatenate([buf[k, slot, half_rows:, columns] for k in slot_z], axis=0)

    def row_block(buf, dx, columns=slice(None)):
        return jnp.concatenate(
            [half_block(buf, 0, block_z[dx], columns), half_block(buf, 1, block_y[dx], columns)], axis=0
        )

    others = [(dx, dc) for dx in nearest_last(nx) + [0] for dc in range(2) if (dx, dc) != (0, 0)]
    barrier = pltpu.get_barrier_semaphore()
    for dx, dc in others:
        pl.semaphore_signal(
            barrier, inc=1, device_id={"mat": x_at[dx], "gc": c_at[dc]}, device_id_type=MESH
        )
    for axis in range(2):
        for to in line[axis][1:]:
            pl.semaphore_signal(barrier, inc=1, device_id={"gr": to}, device_id_type=MESH)
    pl.semaphore_wait(barrier, len(others) + nz - 1 + ny - 1)

    def exchange(dx, dc):
        to_x, to_c = x_at[dx], c_at[dc]
        return pltpu.make_async_remote_copy(
            src_ref=in_ref.at[to_c, :, pl.ds(pl.multiple_of(to_x * width, 128), width)],
            dst_ref=pieces.at[x, c],
            send_sem=a2a_send.at[dx, dc],
            recv_sem=a2a_recv.at[dx, dc],
            device_id={"mat": to_x, "gc": to_c},
            device_id_type=MESH,
        )

    for dx, dc in others:
        exchange(dx, dc).start()
    own = pltpu.make_async_copy(
        in_ref.at[c, :, pl.ds(pl.multiple_of(x * width, 128), width)], pieces.at[x, c], local_sem
    )
    own.start()
    own.wait()
    for dx, dc in others:
        exchange(dx, dc).wait_recv()
    for k in range(nx):
        for core in range(2):
            row = (k * 2 + core) * rpd
            assembled[row : row + rpd, :] = pieces[k, core].astype(jnp.float32)
    block = assembled[...].astype(jnp.bfloat16)
    panel[0, 0] = block

    def owner(half, d):
        return lax.rem(z + d, nz) if half == 0 else lax.rem(y + d, ny)

    def contribute(half, d):
        return pltpu.make_async_remote_copy(
            src_ref=partial.at[half, d],
            dst_ref=partial_in.at[half, x],
            send_sem=rs_send.at[half, d],
            recv_sem=rs_recv.at[half, x],
            device_id={"mat": owner(half, d)},
            device_id_type=MESH,
        )

    def ready(half, d):
        partial[half, d] = lax.dot_general(
            block,
            half_block(panel, half, slot_of(d, nx)),
            (((1,), (1,)), ((), ())),
            preferred_element_type=jnp.float32,
        )

        @pl.when(owner(half, d) != x)
        def _():
            contribute(half, d).start()

        @pl.when(owner(half, d) == x)
        def _():
            partial_in[half, x] = partial[half, d]

    panel_gather = RingGather(panel, (nz, ny), line, pa_send, pa_recv, pb_send, pb_recv)
    panel_gather.run(ready)

    far_first = nearest_last(nx)
    sums = []
    for half in range(2):
        for dx in far_first:
            pltpu.make_async_remote_copy(
                src_ref=partial_in.at[half, x_at[dx]],
                dst_ref=partial_in.at[half, x_at[dx]],
                send_sem=rs_send.at[half, dx],
                recv_sem=rs_recv.at[half, x_at[dx]],
                device_id={"mat": x_at[dx]},
                device_id_type=MESH,
            ).wait_recv()
        total = partial_in[half, 0]
        for k in range(1, nx):
            total = total + partial_in[half, k]
        sums.append(total)
    gram_sum = jnp.concatenate(sums, axis=1)
    gram = (gram_sum * (1.0 / total_cols)).astype(jnp.bfloat16)
    gram_row[0] = gram
    gram_cols[0, 0] = gram

    def spread(buf, send, recv, dx):
        return pltpu.make_async_remote_copy(
            src_ref=buf.at[0],
            dst_ref=buf.at[nx - dx],
            send_sem=send.at[dx],
            recv_sem=recv.at[dx],
            device_id={"mat": x_at[dx]},
            device_id_type=MESH,
        )

    for dx in far_first:
        spread(gram_row, gx_send, gx_recv, dx).start()
    gram_gather = LineGather(gram_cols, (nz, ny), line, ga_send, ga_recv, gb_send, gb_recv)
    gram_gather.run()
    for dx in far_first:
        spread(gram_row, gx_send, gx_recv, dx).wait_recv()

    square = jnp.zeros((block_rows, gram_width), jnp.float32)
    for dx in range(nx):
        square = square + jnp.dot(gram_row[dx], row_block(gram_cols, dx), preferred_element_type=jnp.float32)
    poly_row[0] = (cubic_coef * gram.astype(jnp.float32) + quintic_coef * square).astype(jnp.bfloat16)
    for dx in far_first:
        spread(poly_row, px_send, px_recv, dx).start()

    half_width = width // 2
    low = half_width // 128 * 128
    high = width - low

    def product(start, size, arrives):
        columns = pl.ds(pl.multiple_of(start, 128), size)
        mixed = linear_coef * panel[0, 0, :, columns].astype(jnp.float32)
        for dx in [0] + far_first[::-1]:
            if dx and arrives:
                spread(poly_row, px_send, px_recv, nx - dx).wait_recv()
            mixed = mixed + jnp.dot(
                poly_row[dx], row_block(panel, dx, columns), preferred_element_type=jnp.float32
            )
        return mixed

    first_part = product((1 - c) * low, high, True)

    @pl.when(c == 0)
    def _():
        swap_out[...] = first_part[:, half_width - low :].astype(jnp.bfloat16)

    @pl.when(c == 1)
    def _():
        swap_out[...] = first_part[:, :half_width].astype(jnp.bfloat16)

    swap = pltpu.make_async_remote_copy(
        src_ref=swap_out,
        dst_ref=swap_in,
        send_sem=sw_send,
        recv_sem=sw_recv,
        device_id={"gc": 1 - c},
        device_id_type=MESH,
    )
    swap.start()
    second_part = product(c * high, low, False)

    @pl.when(c == 0)
    def _():
        own_half = jnp.concatenate([second_part, first_part[:, : half_width - low]], axis=1)
        out_ref[0] = own_half.astype(jnp.bfloat16)

    @pl.when(c == 1)
    def _():
        own_half = jnp.concatenate([first_part[:, half_width:], second_part], axis=1)
        out_ref[1] = own_half.astype(jnp.bfloat16)

    for dx, dc in others:
        exchange(dx, dc).wait_send()
    panel_gather.end()
    gram_gather.end()
    for half in range(2):
        for d in range(nx):

            @pl.when(owner(half, d) != x)
            def _():
                contribute(half, d).wait_send()

    for dx in far_first:
        spread(gram_row, gx_send, gx_recv, dx).wait_send()
        spread(poly_row, px_send, px_recv, dx).wait_send()
    swap.wait_recv()
    for core in range(2):

        @pl.when(c == core)
        def _():
            out_ref[1 - core] = swap_in[...]

    swap.wait_send()


def solution(mesh):
    nx, groups = mesh.shape["mat"], mesh.shape["gr"]
    nz = nx
    ny = groups // nz

    def body(iterate):
        mats, _, rpd, total_cols = iterate.shape
        block_rows = rpd * nx * 2
        width = total_cols // nx
        gram_width = ny * block_rows
        dma = pltpu.SemaphoreType.DMA
        long = max(ny, nz)
        return pl.pallas_call(
            functools.partial(kernel, nx, nz, ny, total_cols),
            out_shape=jax.ShapeDtypeStruct((mats, block_rows, width // 2), jnp.bfloat16),
            in_specs=[pl.BlockSpec(memory_space=pl.ANY)],
            out_specs=pl.BlockSpec(memory_space=pltpu.VMEM),
            scratch_shapes=[
                pltpu.VMEM((nx, 2, rpd, width), jnp.bfloat16),
                pltpu.VMEM((block_rows, width), jnp.float32),
                pltpu.VMEM((nz, ny, block_rows, width), jnp.bfloat16),
                pltpu.VMEM((2, nx, block_rows, gram_width // 2), jnp.float32),
                pltpu.VMEM((2, nx, block_rows, gram_width // 2), jnp.float32),
                pltpu.VMEM((nz, ny, block_rows, gram_width), jnp.bfloat16),
                pltpu.VMEM((nx, block_rows, gram_width), jnp.bfloat16),
                pltpu.VMEM((nx, block_rows, gram_width), jnp.bfloat16),
                pltpu.VMEM((block_rows, width // 2), jnp.bfloat16),
                pltpu.VMEM((block_rows, width // 2), jnp.bfloat16),
                dma((nx, 2)),
                dma((nx, 2)),
                dma,
            ]
            + [dma((2, long))] * 2
            + [dma((2, long // 2, 2, 5))] * 2
            + [dma((2, long))] * 4
            + [dma((2, nx))] * 2
            + [dma((nx,))] * 4
            + [dma, dma],
            compiler_params=pltpu.CompilerParams(collective_id=0, has_side_effects=True),
        )(iterate.reshape(mats, rpd, total_cols))

    return jax.shard_map(
        body,
        mesh=mesh,
        in_specs=(P(None, "gr", ("mat", "gc"), None),),
        out_specs=P(None, "gr", ("mat", "gc")),
        check_vma=False,
    )
```
